768 devices in a mesh: dp: 48 (over x, z_lo, core), fsdp: 16 (over y, z_hi).
Axes of the slice: x: 4, y: 8, z: 12 (z_hi: 2, z_lo: 6; z = z_hi * 6 + z_lo), core: 2. Of those that a mesh axis runs over, the one named last changes fastest.
Arguments:
- tokens: bfloat16 [393216, 1024], P(('dp', 'fsdp')), may hold values from -6 to 6
- segments: int32 [393216], P(('dp', 'fsdp')), may hold values from -1 to 1, as said below
- qkv_weight: bfloat16 [1024, 3072], P('fsdp'), may hold values from -6 to 6
- out_weight: bfloat16 [1024, 1024], P('fsdp'), may hold values from -0.1875 to 0.1875
Outputs:
- projected: bfloat16 [393216, 1024], P(('dp', 'fsdp'))
The draws below stay inside these ranges and needn't reach their ends.
Inputs may be any that keep to these rules, and one draw needn't show every extreme that they name: `segments`: each image lies inside one block of 256 rows and is numbered 0 or 1 there; -1 marks empty rows. Each device's 512 rows begin with 0 to 2 blocks that hold images, its other blocks are empty. Two devices with equal fsdp index whose dp indices differ by half the dp axis hold 2 such blocks together; the first device holds 2.
All inputs are finite; a program needn't handle non-finite values.
Results may differ from the reference program's by a relative error of at most 0.0089.
Values may be sent and summed in bfloat16 or wider, within the bound.
No kernel may reach another device: no remote copies, remote signals or barrier semaphores. Data moves between devices by JAX's collectives and lax.ppermute only.
A program may use at most 64 MiB of HBM per device.

```python
import jax
import jax.numpy as jnp
from jax import lax

D = 1024
HEADS = 16
BLK = 256
NB = 2
ROWS_DEV = 512
ROWS = 393216


def draw_segments(key, part):
    device_count = ROWS // ROWS_DEV
    half_count = device_count // 2
    key_count, key_first, key_pad = jax.random.split(key, 3)
    first_half = jax.random.randint(key_count, (half_count,), 0, NB + 1)
    first_half = first_half.at[0].set(NB)
    live_count = jnp.concatenate([first_half, NB - first_half])
    first_len = jax.random.randint(key_first, (device_count, NB), BLK // 4, BLK // 2 + 1)
    padding = jax.random.randint(key_pad, (device_count, NB), 0, BLK // 4)
    second_end = BLK - padding
    position = jnp.arange(BLK)[None, None, :]
    image_ids = jnp.where(position < first_len[..., None], 0, jnp.where(position < second_end[..., None], 1, -1))
    live_block = jnp.arange(NB)[None, :] < live_count[:, None]
    image_ids = jnp.where(live_block[..., None], image_ids, -1)
    return image_ids.reshape(ROWS).astype(jnp.int32)


def draw_qkv_weight(key, part):
    spread = D ** (-0.5)
    return (jax.random.normal(key, (D, 3 * D), jnp.float32) * spread).astype(jnp.bfloat16)


def block_levels(stream_key, dims, cuts, least, top_value):
    factor_of, own = 1.0, jax.random.fold_in(stream_key, 6)
    for dim, parts in cuts:
        draws = jnp.exp(jax.random.uniform(jax.random.fold_in(own, dim), (parts,), jnp.float32, least / len(cuts), top_value / len(cuts)))
        factor_of = factor_of * jnp.repeat(draws, dims[dim] // parts).reshape([-1 if axis == dim else 1 for axis in range(len(dims))])
    return factor_of


def normal_values(rng, shape, scale, bound, shards=(), held_as=jnp.bfloat16):
    values = scale * jax.random.normal(rng, shape, jnp.float32)
    if shards:
        values = values * block_levels(rng, shape, shards, -0.22, 0.18)
    return jnp.clip(values, -bound, bound).astype(held_as)


def setup_inputs(seed: int = 0) -> dict:
    key_of = jax.random.split(jax.random.key(seed), 5)
    return {
        "tokens": normal_values(key_of[0], (ROWS, D), 1.0, 6.0, ((0, 768),)),
        "segments": draw_segments(jax.random.fold_in(key_of[4], 71), 0),
        "qkv_weight": draw_qkv_weight(jax.random.fold_in(key_of[4], 71), 0),
        "out_weight": normal_values(key_of[3], (D, D), D ** -0.5, 0.1875, ((0, 16),)),
    }


def normalize(block_rows):
    values_f = block_rows.astype(jnp.float32)
    row_mean = lax.optimization_barrier(jnp.mean(values_f, axis=-1, keepdims=True))
    centered = values_f - row_mean
    variance = lax.optimization_barrier(jnp.mean(centered * centered, axis=-1, keepdims=True))
    return (centered * lax.rsqrt(variance + 1e-05)).astype(jnp.bfloat16)

def attend(packed_qkv, segment, head_count):
    row_count = packed_qkv.shape[0]
    model_width = packed_qkv.shape[1] // 3
    head_dim = model_width // head_count
    queries = packed_qkv[:, :model_width].reshape(row_count, head_count, head_dim).astype(jnp.float32)
    key_rows = packed_qkv[:, model_width:2 * model_width].reshape(row_count, head_count, head_dim).astype(jnp.float32)
    values = packed_qkv[:, 2 * model_width:].reshape(row_count, head_count, head_dim).astype(jnp.float32)
    scores = jnp.einsum('qhd,khd->hqk', queries, key_rows) * head_dim ** (-0.5)
    same_image = segment[:, None] == segment[None, :]
    scores = jnp.where(same_image[None], scores, -1e+30)
    row_max = lax.optimization_barrier(jnp.max(scores, axis=-1, keepdims=True))
    weights = jnp.exp(scores - row_max)
    row_total = lax.optimization_barrier(jnp.sum(weights, axis=-1, keepdims=True))
    attention = (weights / row_total).astype(jnp.bfloat16)
    mixed_rows = jnp.einsum('hqk,khd->qhd', attention.astype(jnp.float32), values)
    return mixed_rows.reshape(row_count, model_width).astype(jnp.bfloat16)

def sublayer(token_rows, segment, qkv_weight, out_weight):
    normed = normalize(token_rows)
    packed_qkv = jnp.dot(normed, qkv_weight, preferred_element_type=jnp.float32).astype(jnp.bfloat16)
    mixed_rows = attend(packed_qkv, segment, HEADS)
    result = jnp.dot(mixed_rows, out_weight, preferred_element_type=jnp.float32)
    return jnp.where(segment[:, None] >= 0, result, 0.0).astype(jnp.bfloat16)

def reference(tokens, segments, qkv_weight, out_weight):
    block_count = ROWS // BLK
    block_tokens = tokens.reshape(block_count, BLK, D)
    block_segments = segments.reshape(block_count, BLK)

    def one_block(operands):
        return sublayer(operands[0], operands[1], qkv_weight, out_weight)
    out_blocks = lax.map(one_block, (block_tokens, block_segments))
    return out_blocks.reshape(ROWS, D)
```

```python
import functools

import jax
import jax.numpy as jnp
from jax import lax
from jax.experimental import pallas as pl
from jax.experimental.pallas import tpu as pltpu
from jax.sharding import PartitionSpec as P

HEADS = 16
BLK = 256
HD = 64
D = 1024
X, ZL, CORES, ZH = 4, 6, 2, 2
PIECE = 128
QKV = 3 * PIECE
EXP_SCALE = HD ** (-0.5) * 1.4426950408889634


def normalize(block_rows):
    values_f = block_rows.astype(jnp.float32)
    row_mean = jnp.mean(values_f, axis=-1, keepdims=True)
    centered = values_f - row_mean
    variance = jnp.mean(centered * centered, axis=-1, keepdims=True)
    return (centered * lax.rsqrt(variance + 1e-05)).astype(jnp.bfloat16)


def attend_kernel(normed_ref, wa_ref, wb_ref, segc_ref, segr_ref, oa_ref, ob_ref):
    for b in range(2):
        rows = pl.ds(b * BLK, BLK)
        live = jnp.max(segr_ref[b : b + 1, :]) >= 0

        @pl.when(live)
        def _():
            normed = normed_ref[rows, :]
            same = segc_ref[rows, :] == segr_ref[b : b + 1, :]
            for w_ref, o_ref in ((wa_ref, oa_ref), (wb_ref, ob_ref)):
                qkv = jnp.dot(
                    normed, w_ref[...], preferred_element_type=jnp.float32
                ).astype(jnp.bfloat16)
                mixed = []
                for h in range(2):
                    q = qkv[:, h * HD : (h + 1) * HD]
                    k = qkv[:, PIECE + h * HD : PIECE + (h + 1) * HD]
                    v = qkv[:, 2 * PIECE + h * HD : 2 * PIECE + (h + 1) * HD]
                    s = lax.dot_general(
                        q, k, (((1,), (1,)), ((), ())), preferred_element_type=jnp.float32
                    )
                    s = jnp.where(same, s, -1e30)
                    m = jnp.max(s, axis=-1, keepdims=True)
                    p = jnp.exp2((s - m) * EXP_SCALE)
                    total = jnp.sum(p, axis=-1, keepdims=True)
                    o = jnp.dot(
                        p.astype(jnp.bfloat16), v, preferred_element_type=jnp.float32
                    )
                    mixed.append(o / total)
                o_ref[rows, :] = jnp.concatenate(mixed, axis=1).astype(jnp.bfloat16)

        @pl.when(jnp.logical_not(live))
        def _():
            oa_ref[rows, :] = jnp.zeros((BLK, PIECE), jnp.bfloat16)
            ob_ref[rows, :] = jnp.zeros((BLK, PIECE), jnp.bfloat16)


def attend(normed, wa, wb, segc, segr):
    rows = normed.shape[0]
    full = lambda shape: pl.BlockSpec(shape, lambda i: (0, 0))
    return pl.pallas_call(
        attend_kernel,
        grid=(1,),
        in_specs=[
            full((rows, D)),
            full((D, QKV)),
            full((D, QKV)),
            full((rows, 1)),
            full((2, BLK)),
        ],
        out_specs=[full((rows, PIECE)), full((rows, PIECE))],
        out_shape=[jax.ShapeDtypeStruct((rows, PIECE), jnp.bfloat16)] * 2,
        compiler_params=pltpu.CompilerParams(vmem_limit_bytes=20 << 20),
        cost_estimate=pl.CostEstimate(
            flops=2 * rows * D * 2 * QKV + 8 * rows * BLK * 2 * PIECE,
            transcendentals=4 * rows * BLK,
            bytes_accessed=4 * D * QKV,
        ),
    )(normed, wa, wb, segc, segr)


def project_kernel(where_ref, segc_ref, *refs):
    mixed_refs, w_refs, out_ref, mixed_all = refs[:8], refs[8:16], refs[16], refs[17]
    for j in range(8):
        cols = pl.ds(pl.multiple_of(where_ref[j] * PIECE, PIECE), PIECE)
        mixed_all[:, cols] = mixed_refs[j][...]
    keep = segc_ref[...] >= 0
    for j in range(8):
        cols = pl.ds(pl.multiple_of(where_ref[j] * PIECE, PIECE), PIECE)
        result = jnp.dot(mixed_all[...], w_refs[j][...], preferred_element_type=jnp.float32)
        out_ref[:, cols] = jnp.where(keep, result, 0.0).astype(jnp.bfloat16)


def project(where, segc, mixed, weights):
    rows = segc.shape[0]
    full = lambda shape: pl.BlockSpec(shape, lambda i, w: (0, 0))
    return pl.pallas_call(
        project_kernel,
        grid_spec=pltpu.PrefetchScalarGridSpec(
            num_scalar_prefetch=1,
            grid=(1,),
            in_specs=[full((rows, 1))]
            + [full((rows, PIECE))] * 8
            + [pl.BlockSpec((D, PIECE), lambda i, w: (0, 3))] * 8,
            out_specs=full((rows, D)),
            scratch_shapes=[pltpu.VMEM((rows, D), jnp.bfloat16)],
        ),
        out_shape=jax.ShapeDtypeStruct((rows, D), jnp.bfloat16),
        compiler_params=pltpu.CompilerParams(vmem_limit_bytes=24 << 20),
        cost_estimate=pl.CostEstimate(
            flops=2 * rows * D * D, transcendentals=0, bytes_accessed=2 * D * D + 4 * rows * D
        ),
    )(where, segc, *mixed, *weights)


def next_z(dp, fsdp):
    core, zl, x = dp % CORES, dp // CORES % ZL, dp // (CORES * ZL)
    zh, y = fsdp % ZH, fsdp // ZH
    if zl < ZL - 1:
        zl += 1
    else:
        zl, zh = 0, 1 - zh
    return (x * ZL + zl) * CORES + core, y * ZH + zh


def body(n_dp, n_fsdp, tokens, segments, qkv_weight, out_weight):
    dp = lax.axis_index("dp")
    core = dp % CORES
    colour = (dp // (CORES * ZL) + 2 * (dp // CORES % ZL % 2)) % 4
    mine = colour * 2 + core

    take = lambda w, start: lax.dynamic_slice_in_dim(w, start, PIECE, axis=1)
    part = jnp.concatenate(
        [take(qkv_weight, mine * PIECE + j * D) for j in range(3)]
        + [take(out_weight, mine * PIECE)],
        axis=1,
    )
    piece = lax.all_to_all(jnp.tile(part, (n_fsdp, 1)), "fsdp", 0, 0, tiled=True)

    step = CORES * ZL
    x_up = [(i, (i + step) % n_dp) for i in range(n_dp)]
    x_down = [(i, (i - step) % n_dp) for i in range(n_dp)]
    z_up = []
    for i in range(n_dp):
        for j in range(n_fsdp):
            to_dp, to_fsdp = next_z(i, j)
            z_up.append((i * n_fsdp + j, to_dp * n_fsdp + to_fsdp))
    swap = [(i, i ^ 1) for i in range(n_dp)]

    pieces = [
        (piece, colour),
        (lax.ppermute(piece, "dp", x_up), (colour + 3) % 4),
        (lax.ppermute(piece, "dp", x_down), (colour + 1) % 4),
        (lax.ppermute(piece, ("dp", "fsdp"), z_up), (colour + 2) % 4),
    ]

    normed = normalize(tokens)
    segc = segments[:, None]
    segr = segments.reshape(2, BLK)
    mixed, weights, where = [], [], []
    for own, c in pieces:
        other = lax.ppermute(own, "dp", swap)
        mixed += attend(normed, own, other, segc, segr)
        weights += [own, other]
        where += [c * 2 + core, c * 2 + 1 - core]
    return project(jnp.stack(where).astype(jnp.int32), segc, mixed, weights)


def solution(mesh):
    return jax.shard_map(
        functools.partial(body, mesh.shape["dp"], mesh.shape["fsdp"]),
        mesh=mesh,
        in_specs=(P(("dp", "fsdp"), None), P(("dp", "fsdp")), P("fsdp", None), P("fsdp", None)),
        out_specs=P(("dp", "fsdp"), None),
        check_vma=False,
    )
```
